32 devices in a mesh: dp: 8 (over z, y), tensor: 4 (over x, core).
Axes of the slice: x: 2, y: 2, z: 4, core: 2. Of those that a mesh axis runs over, the one named last changes fastest.
Arguments:
- tokens: bfloat16 [8, 512, 768], P('dp'), as said below
- cotangent: bfloat16 [8, 512, 768], P('dp'), may hold values from -6 to 6
- lengths: int32 [8], P('dp'), may hold values from 128 to 512, as said below
- in_weight: float32 [7, 768, 768], P(None, 'dp', 'tensor'), as said below
- out_weight: float32 [5, 768, 768], P(None, 'tensor', 'dp'), may hold values from -0.4375 to 0.4375
- in_bias: float32 [6, 768], P(None, 'tensor'), may hold values from -3 to 3
- norm_vec: float32 [6, 768], replicated, may hold values from 0.1 to 1.9
- in_moments: float32 [2, 7, 768, 768], P(None, None, 'dp', 'tensor'), as said below
- out_moments: float32 [2, 5, 768, 768], P(None, None, 'tensor', 'dp'), as said below
- bias_moments: float32 [2, 6, 768], P(None, None, 'tensor'), as said below
- norm_moments: float32 [2, 6, 768], replicated, as said below
Outputs:
- output: bfloat16 [8, 512, 768], P('dp')
- grad_input: bfloat16 [8, 512, 768], P('dp')
- in_grad: float32 [7, 768, 768], P(None, 'dp', 'tensor')
- out_grad: float32 [5, 768, 768], P(None, 'tensor', 'dp')
- bias_grad: float32 [6, 768], P(None, 'tensor')
- norm_grad: float32 [6, 768], replicated
- new_in_weight: float32 [7, 768, 768], P(None, 'dp', 'tensor')
- new_out_weight: float32 [5, 768, 768], P(None, 'tensor', 'dp')
- new_in_bias: float32 [6, 768], P(None, 'tensor')
- new_norm_vec: float32 [6, 768], replicated
- new_in_moments: float32 [2, 7, 768, 768], P(None, None, 'dp', 'tensor')
- new_out_moments: float32 [2, 5, 768, 768], P(None, None, 'tensor', 'dp')
- new_bias_moments: float32 [2, 6, 768], P(None, None, 'tensor')
- new_norm_moments: float32 [2, 6, 768], replicated
The draws below stay inside these ranges and needn't reach their ends.
Inputs may be any that keep to these rules, and one draw needn't show every extreme that they name: `lengths`: each sequence's live tokens come first; the first sequence is full, with 512 live tokens. `tokens`: entries lie within -6 and 6. `in_weight`: entries lie within -6 / sqrt(768) and 6 / sqrt(768). `in_moments`: second moments (index 1) are positive. `out_moments`: second moments (index 1) are positive. `bias_moments`: second moments (index 1) are positive. `norm_moments`: second moments (index 1) are positive.
All inputs are finite; a program needn't handle non-finite values.
Results may differ from the reference program's by a relative error of at most 0.023.
Values may be sent and summed in bfloat16 or wider, within the bound.
A program may use at most 128 MiB of HBM per device.

```python
import math
import jax
import jax.numpy as jnp
from jax import lax

D = 768
HEADS = 12
HDIM = 64
SEQ_LEN = 512
SEQ_DEV = 1
SEQS = 8
N_TENSOR = 4


token_bound = 6.0


def draw_tokens(key, part):
    base = jnp.clip(jax.random.normal(jax.random.fold_in(key, 31), (SEQS, SEQ_LEN, D), jnp.float32), -token_bound, token_bound)
    return base.astype(jnp.bfloat16)


def draw_in_weight(key, part):
    base = jnp.clip(jax.random.normal(jax.random.fold_in(key, 32), (7, D, D), jnp.float32), -token_bound, token_bound) * D ** (-0.5)
    return base


def draw_lengths(key, part):
    devices = SEQS // SEQ_DEV
    key_base = jax.random.fold_in(key, 11)
    key_factor = jax.random.fold_in(key, 12)
    lowest = max(1, SEQ_LEN // 4)
    base = jax.random.randint(key_base, (devices, SEQ_DEV), lowest, SEQ_LEN // 2 + 1)
    factor = jax.random.randint(key_factor, (devices, 1), 1, 3)
    sizes = jnp.minimum(base * factor, SEQ_LEN).reshape(SEQS)
    return sizes.at[0].set(SEQ_LEN).astype(jnp.int32)


def moment_pair(key, shape, salt):
    own_key = jax.random.fold_in(key, salt)
    key_first = jax.random.fold_in(own_key, 21)
    key_second = jax.random.fold_in(own_key, 22)
    first = 5.0 * jax.random.normal(key_first, shape, jnp.float32)
    second = jnp.exp(jax.random.uniform(key_second, shape, jnp.float32, math.log(0.5), math.log(20.0)))
    return jnp.stack([first, second])


def draw_in_moments(key, part):
    return moment_pair(key, (7, D, D), 101)


def draw_out_moments(key, part):
    return moment_pair(key, (5, D, D), 102)


def draw_bias_moments(key, part):
    return moment_pair(key, (6, D), 103)


def draw_norm_moments(key, part):
    return moment_pair(key, (6, D), 104)


def block_scale(key, dims, pieces, least, high):
    loudness = 1.0
    for axis_at, parts in pieces:
        heights = jax.random.uniform(jax.random.fold_in(jax.random.fold_in(key, 6), axis_at), (parts,), jnp.float32, least / len(pieces), high / len(pieces))
        loudness = loudness * jnp.repeat(jnp.exp(heights), dims[axis_at] // parts).reshape((-1,) + (1,) * (len(dims) - 1 - axis_at))
    return loudness


def scatter_about(key, shape, width, most, shards=(), kind=jnp.bfloat16):
    result = jax.random.normal(key, shape, jnp.float32) * width
    if len(shards) > 0:
        result = block_scale(key, shape, shards, -0.22, 0.18) * result
    return jnp.clip(result, min=-most, max=most).astype(kind)


def setup_inputs(seed: int = 0) -> dict:
    streams_of = jax.random.split(jax.random.key(seed), 12)
    tokens = draw_tokens(jax.random.fold_in(streams_of[11], 71), 0)
    cotangent = scatter_about(streams_of[1], (SEQS, SEQ_LEN, D), 1.0, 6.0, ((0, 8),))
    lengths = draw_lengths(jax.random.fold_in(streams_of[11], 71), 0)
    in_weight = draw_in_weight(jax.random.fold_in(streams_of[11], 71), 0)
    out_weight = scatter_about(streams_of[4], (5, D, D), (D // 4) ** -0.5, 0.4375, ((1, 4), (2, 8)), jnp.float32)
    in_bias = scatter_about(streams_of[5], (6, D), 0.5, 3.0, ((1, 4),), jnp.float32)
    norm_vec = jnp.clip(1.0 + 0.18 * jax.random.normal(streams_of[6], (6, D), jnp.float32), 0.1, 1.9)
    in_moments = draw_in_moments(jax.random.fold_in(streams_of[11], 71), 0)
    out_moments = draw_out_moments(jax.random.fold_in(streams_of[11], 71), 0)
    bias_moments = draw_bias_moments(jax.random.fold_in(streams_of[11], 71), 0)
    norm_moments = draw_norm_moments(jax.random.fold_in(streams_of[11], 71), 0)
    return {"tokens": tokens, "cotangent": cotangent, "lengths": lengths, "in_weight": in_weight, "out_weight": out_weight, "in_bias": in_bias, "norm_vec": norm_vec, "in_moments": in_moments, "out_moments": out_moments, "bias_moments": bias_moments, "norm_moments": norm_moments}


norm_eps = 1e-12
masked_score = -1e+30
learn_rate = 0.005
beta_first = 0.9
beta_second = 0.999
adam_eps = 1e-08
weight_decay = 0.01
step_count = 2.0
root_half = 0.7071067811865476
normal_peak = 0.3989422804014327

def matmul(left_op, right_op):
    return jnp.dot(left_op, right_op, preferred_element_type=jnp.float32)

def rounded_wide(values):
    return lax.optimization_barrier(values.astype(jnp.bfloat16)).astype(jnp.float32)

def layer_norm(summed_rows, gain_vec, shift_vec):
    center = lax.optimization_barrier(jnp.mean(summed_rows, -1, keepdims=True))
    offset = summed_rows - center
    inverse = lax.rsqrt(lax.optimization_barrier(jnp.mean(offset * offset, -1, keepdims=True)) + norm_eps)
    normed = offset * inverse
    return (normed * gain_vec + shift_vec, normed, inverse)

def norm_back(upstream, normed, inverse, gain_vec):
    scaled = upstream * gain_vec
    return inverse * (scaled - lax.optimization_barrier(jnp.mean(scaled, -1, keepdims=True)) - normed * lax.optimization_barrier(jnp.mean(scaled * normed, -1, keepdims=True)))

def gelu_value(pre_act):
    return 0.5 * pre_act * (1.0 + jax.scipy.special.erf(pre_act * root_half))

def gelu_slope(pre_act):
    return 0.5 * (1.0 + jax.scipy.special.erf(pre_act * root_half)) + pre_act * jnp.exp(-0.5 * pre_act * pre_act) * normal_peak

def tensor_sum(partials):
    return lax.optimization_barrier(jnp.sum(rounded_wide(partials), 0))

def adam_update(param, grad, moments, decay):
    first = beta_first * moments[0] + (1.0 - beta_first) * grad
    second = beta_second * moments[1] + (1.0 - beta_second) * grad * grad
    first_hat = first / (1.0 - beta_first ** step_count)
    second_hat = second / (1.0 - beta_second ** step_count)
    new_param = param - learn_rate * (first_hat / (jnp.sqrt(second_hat) + adam_eps) + decay * param)
    return (new_param, jnp.stack([first, second]))

def reference(tokens, cotangent, lengths, in_weight, out_weight, in_bias, norm_vec, in_moments, out_moments, bias_moments, norm_moments):
    group_width = D // N_TENSOR
    in_low = in_weight.astype(jnp.bfloat16)
    out_low = out_weight.astype(jnp.bfloat16)
    w_query, w_key, w_value = (in_low[0], in_low[1], in_low[2])
    w_proj = out_low[0]
    up_wide = in_low[3:7].astype(jnp.float32)
    down_wide = out_low[1:5].astype(jnp.float32)
    up_groups = up_wide.reshape(4, D, N_TENSOR, group_width)
    down_groups = down_wide.reshape(4, N_TENSOR, group_width, D)
    proj_groups = w_proj.astype(jnp.float32).reshape(N_TENSOR, group_width, D)
    query_groups = w_query.astype(jnp.float32).reshape(D, N_TENSOR, group_width)
    key_groups = w_key.astype(jnp.float32).reshape(D, N_TENSOR, group_width)
    value_groups = w_value.astype(jnp.float32).reshape(D, N_TENSOR, group_width)
    scale_factor = HDIM ** (-0.5)

    def one_sequence(carry, operands):
        seq_tokens, seq_cot, length = operands
        positions = lax.broadcasted_iota(jnp.int32, (SEQ_LEN,), 0)
        usable = positions < length
        live_rows = usable.astype(jnp.float32)
        query = (matmul(seq_tokens, w_query) + in_bias[0]).astype(jnp.bfloat16)
        keys_low = matmul(seq_tokens, w_key).astype(jnp.bfloat16)
        values_low = (matmul(seq_tokens, w_value) + in_bias[1]).astype(jnp.bfloat16)
        query_heads = query.astype(jnp.float32).reshape(SEQ_LEN, HEADS, HDIM)
        key_heads = keys_low.astype(jnp.float32).reshape(SEQ_LEN, HEADS, HDIM)
        value_heads = values_low.astype(jnp.float32).reshape(SEQ_LEN, HEADS, HDIM)
        scores = jnp.einsum('qhe,khe->hqk', query_heads, key_heads) * scale_factor
        scores = jnp.where(usable[None, None, :], scores, masked_score)
        highest = lax.optimization_barrier(jnp.max(scores, -1, keepdims=True))
        log_total = highest + jnp.log(lax.optimization_barrier(jnp.sum(jnp.exp(scores - highest), -1, keepdims=True)))
        probs = jnp.exp(scores - log_total)
        probs_low = rounded_wide(probs)
        mixed = jnp.einsum('hqk,khe->qhe', probs_low, value_heads).reshape(SEQ_LEN, D).astype(jnp.bfloat16)
        mixed_wide = mixed.astype(jnp.float32)
        attn = tensor_sum(jnp.einsum('ltc,tcd->tld', mixed_wide.reshape(SEQ_LEN, N_TENSOR, group_width), proj_groups))
        hidden, normed_one, inverse_one = layer_norm(seq_tokens.astype(jnp.float32) + attn + norm_vec[0], norm_vec[1], norm_vec[2])
        hidden_low = hidden.astype(jnp.bfloat16)
        hidden_wide = hidden_low.astype(jnp.float32)
        pre_act = jnp.einsum('ld,kdc->lkc', hidden_wide, up_wide) + in_bias[2:6]
        act_low = gelu_value(pre_act).astype(jnp.bfloat16)
        act_wide = act_low.astype(jnp.float32)
        ffn = tensor_sum(jnp.einsum('lktj,ktjd->tld', act_wide.reshape(SEQ_LEN, 4, N_TENSOR, group_width), down_groups))
        out_rows, normed_two, inverse_two = layer_norm(hidden + ffn + norm_vec[3], norm_vec[4], norm_vec[5])
        grad_out = seq_cot.astype(jnp.float32) * live_rows[:, None]
        grad_two = norm_back(grad_out, normed_two, inverse_two, norm_vec[4])
        grad_two_low = grad_two.astype(jnp.bfloat16)
        grad_two_wide = grad_two_low.astype(jnp.float32)
        grad_act = jnp.einsum('ld,kcd->lkc', grad_two_wide, down_wide)
        grad_pre = grad_act * gelu_slope(pre_act)
        grad_pre_low = grad_pre.astype(jnp.bfloat16)
        grad_pre_wide = grad_pre_low.astype(jnp.float32)
        grad_hidden = grad_two + tensor_sum(jnp.einsum('lktj,kdtj->tld', grad_pre_wide.reshape(SEQ_LEN, 4, N_TENSOR, group_width), up_groups))
        grad_one = norm_back(grad_hidden, normed_one, inverse_one, norm_vec[1])
        grad_one_low = grad_one.astype(jnp.bfloat16)
        grad_mixed = jnp.dot(grad_one_low, w_proj.T, preferred_element_type=jnp.float32).astype(jnp.bfloat16)
        grad_heads = grad_mixed.astype(jnp.float32).reshape(SEQ_LEN, HEADS, HDIM)
        grad_probs = jnp.einsum('qhe,khe->hqk', grad_heads, value_heads)
        row_dot = lax.optimization_barrier(jnp.sum(probs * grad_probs, -1, keepdims=True))
        grad_scores = rounded_wide(probs * (grad_probs - row_dot) * scale_factor)
        grad_query = jnp.einsum('hqk,khe->qhe', grad_scores, key_heads).reshape(SEQ_LEN, D)
        grad_keys = jnp.einsum('hqk,qhe->khe', grad_scores, query_heads).reshape(SEQ_LEN, D)
        grad_values = jnp.einsum('hqk,qhe->khe', probs_low, grad_heads).reshape(SEQ_LEN, D)
        query_low = grad_query.astype(jnp.bfloat16)
        keys_grad_low = grad_keys.astype(jnp.bfloat16)
        values_grad_low = grad_values.astype(jnp.bfloat16)
        input_parts = jnp.einsum('ltj,dtj->tld', query_low.astype(jnp.float32).reshape(SEQ_LEN, N_TENSOR, group_width), query_groups)
        input_parts = input_parts + jnp.einsum('ltj,dtj->tld', keys_grad_low.astype(jnp.float32).reshape(SEQ_LEN, N_TENSOR, group_width), key_groups)
        input_parts = input_parts + jnp.einsum('ltj,dtj->tld', values_grad_low.astype(jnp.float32).reshape(SEQ_LEN, N_TENSOR, group_width), value_groups)
        grad_input = (grad_one + tensor_sum(input_parts)).astype(jnp.bfloat16)
        grad_up = jnp.einsum('ld,lkc->kdc', hidden_wide, grad_pre_wide)
        grad_in = jnp.concatenate([jnp.stack([matmul(seq_tokens.T, query_low), matmul(seq_tokens.T, keys_grad_low), matmul(seq_tokens.T, values_grad_low)]), grad_up], 0)
        grad_down = jnp.einsum('lkc,ld->kcd', act_wide, grad_two_wide)
        grad_outw = jnp.concatenate([matmul(mixed.T, grad_one_low)[None], grad_down], 0)
        grad_bias = jnp.concatenate([jnp.stack([lax.optimization_barrier(jnp.sum(grad_query, 0)), lax.optimization_barrier(jnp.sum(grad_values, 0))]), lax.optimization_barrier(jnp.sum(grad_pre, 0))], 0)
        grad_norm = jnp.stack([lax.optimization_barrier(jnp.sum(grad_one, 0)), lax.optimization_barrier(jnp.sum(grad_hidden * normed_one, 0)), lax.optimization_barrier(jnp.sum(grad_hidden, 0)), lax.optimization_barrier(jnp.sum(grad_two, 0)), lax.optimization_barrier(jnp.sum(grad_out * normed_two, 0)), lax.optimization_barrier(jnp.sum(grad_out, 0))])
        new_carry = (carry[0] + grad_in, carry[1] + grad_outw, carry[2] + grad_bias, carry[3] + grad_norm)
        return (new_carry, (out_rows.astype(jnp.bfloat16), grad_input))
    start = (jnp.zeros((7, D, D), jnp.float32), jnp.zeros((5, D, D), jnp.float32), jnp.zeros((6, D), jnp.float32), jnp.zeros((6, D), jnp.float32))
    totals, outputs = lax.scan(one_sequence, start, (tokens, cotangent, lengths))
    in_grad, out_grad, bias_grad, norm_grad = totals
    new_in_weight, new_in_moments = adam_update(in_weight, in_grad, in_moments, weight_decay)
    new_out_weight, new_out_moments = adam_update(out_weight, out_grad, out_moments, weight_decay)
    new_in_bias, new_bias_moments = adam_update(in_bias, bias_grad, bias_moments, 0.0)
    new_norm_vec, new_norm_moments = adam_update(norm_vec, norm_grad, norm_moments, 0.0)
    return (outputs[0], outputs[1], in_grad, out_grad, bias_grad, norm_grad, new_in_weight, new_out_weight, new_in_bias, new_norm_vec, new_in_moments, new_out_moments, new_bias_moments, new_norm_moments)
```

```python
import functools

import jax
import jax.numpy as jnp
from jax import lax
from jax.experimental import pallas as pl
from jax.experimental.pallas import tpu as pltpu
from jax.sharding import PartitionSpec as P

HDIM = 64


norm_eps = 1e-12
masked_score = -1e30
learn_rate = 0.005
beta_first = 0.9
beta_second = 0.999
adam_eps = 1e-08
weight_decay = 0.01
step_count = 2.0
root_half = 0.7071067811865476
normal_peak = 0.3989422804014327


RING = 8
MESH = pl.DeviceIdType.MESH


def ring_place(index):
    depth, side = index // 2, index % 2
    return depth + side * (RING - 1 - 2 * depth)


def ring_device(place):
    side = place // (RING // 2)
    depth = place + side * (RING - 1 - 2 * place)
    return 2 * depth + side


def ring_neighbours():
    me = lax.axis_index("dp")
    place = ring_place(me)
    right = ring_device((place + 1) % RING)
    left = ring_device((place + RING - 1) % RING)
    return me, place, (right, left)


def greet(axis, devices):
    barrier = pltpu.get_barrier_semaphore()
    for device in devices:
        pl.semaphore_signal(barrier, inc=1, device_id={axis: device}, device_id_type=MESH)
    pl.semaphore_wait(barrier, len(devices))


PIECES = 2


def gather_kernel(share_ref, full_ref, local_sem, send_sem, recv_sem):
    me, place, targets = ring_neighbours()
    rows, columns = share_ref.shape
    piece_rows, half = rows // PIECES, columns // 2

    def full_at(owner, piece, way):
        start = pl.multiple_of(owner * rows + piece * piece_rows, piece_rows)
        return full_ref.at[pl.ds(start, piece_rows), pl.ds(way * half, half)]

    own_start = pl.multiple_of(me * rows, rows)
    own = pltpu.make_async_copy(share_ref, full_ref.at[pl.ds(own_start, rows)], local_sem)
    own.start()
    greet("dp", targets)
    copies = {}
    for step in range(RING - 1):
        for piece in range(PIECES):
            for way in range(2):
                if step:
                    copies[step - 1, piece, way].wait_recv()
                shift = RING - step if way == 0 else step
                owner = ring_device((place + shift) % RING)
                target = full_at(owner, piece, way)
                source = target
                if step == 0:
                    source = share_ref.at[
                        pl.ds(piece * piece_rows, piece_rows), pl.ds(way * half, half)
                    ]
                copy = pltpu.make_async_remote_copy(
                    src_ref=source,
                    dst_ref=target,
                    send_sem=send_sem.at[step, piece, way],
                    recv_sem=recv_sem.at[step, piece, way],
                    device_id={"dp": targets[way]},
                    device_id_type=MESH,
                )
                copy.start()
                copies[step, piece, way] = copy
    for (step, piece, way), copy in copies.items():
        copy.wait_send()
        if step == RING - 2:
            copy.wait_recv()
    own.wait()


def ring_gather(share):
    rows, columns = share.shape
    return pl.pallas_call(
        gather_kernel,
        out_shape=jax.ShapeDtypeStruct((rows * RING, columns), share.dtype),
        in_specs=[pl.BlockSpec(memory_space=pltpu.VMEM)],
        out_specs=pl.BlockSpec(memory_space=pltpu.VMEM),
        scratch_shapes=[
            pltpu.SemaphoreType.DMA,
            pltpu.SemaphoreType.DMA((RING - 1, PIECES, 2)),
            pltpu.SemaphoreType.DMA((RING - 1, PIECES, 2)),
        ],
        compiler_params=pltpu.CompilerParams(collective_id=0, has_side_effects=True),
    )(share)


def scatter_kernel(
    grad_ref,
    small_ref,
    share_ref,
    small_out_ref,
    arrived,
    leaving,
    small_slots,
    send_sem,
    recv_sem,
    small_send,
    small_recv,
):
    me, place, targets = ring_neighbours()
    rows, columns = share_ref.shape
    piece_rows, half = rows // PIECES, columns // 2
    greet("dp", [(me + shift) % RING for shift in range(1, RING)])

    def grad_at(owner, piece, way):
        start = pl.multiple_of(owner * rows + piece * piece_rows, piece_rows)
        return grad_ref.at[pl.ds(start, piece_rows), pl.ds(way * half, half)]

    copies = {}
    small_copies = []
    for step in range(RING - 1):
        for piece in range(PIECES):
            for way in range(2):
                shift = RING - 1 - step if way == 0 else 1 + step
                source = grad_at(ring_device((place + shift) % RING), piece, way)
                if step:
                    copies[step - 1, piece, way].wait_recv()
                    running = arrived[step - 1, piece, way].astype(jnp.float32)
                    running += source[...].astype(jnp.float32)
                    leaving[step, piece, way] = running.astype(jnp.bfloat16)
                    source = leaving.at[step, piece, way]
                copy = pltpu.make_async_remote_copy(
                    src_ref=source,
                    dst_ref=arrived.at[step, piece, way],
                    send_sem=send_sem.at[step, piece, way],
                    recv_sem=recv_sem.at[step, piece, way],
                    device_id={"dp": targets[way]},
                    device_id_type=MESH,
                )
                copy.start()
                copies[step, piece, way] = copy
        if step == 0:
            for shift in range(1, RING):
                copy = pltpu.make_async_remote_copy(
                    src_ref=small_ref,
                    dst_ref=small_slots.at[me],
                    send_sem=small_send.at[shift - 1],
                    recv_sem=small_recv.at[shift - 1],
                    device_id={"dp": (me + shift) % RING},
                    device_id_type=MESH,
                )
                copy.start()
                small_copies.append(copy)
    for piece in range(PIECES):
        for way in range(2):
            copies[RING - 2, piece, way].wait_recv()
            total = arrived[RING - 2, piece, way].astype(jnp.float32)
            total += grad_at(me, piece, way)[...].astype(jnp.float32)
            share_ref[pl.ds(piece * piece_rows, piece_rows), pl.ds(way * half, half)] = total
    for copy in small_copies:
        copy.wait_recv()
    small_slots[me] = small_ref[...]
    small_total = small_slots[0]
    for index in range(1, RING):
        small_total += small_slots[index]
    small_out_ref[...] = small_total
    for copy in small_copies:
        copy.wait_send()
    for copy in copies.values():
        copy.wait_send()


def ring_scatter(grads, small):
    rows, columns = grads.shape[0] // RING, grads.shape[1]
    slot_shape = (RING - 1, PIECES, 2, rows // PIECES, columns // 2)
    vmem = pl.BlockSpec(memory_space=pltpu.VMEM)
    return pl.pallas_call(
        scatter_kernel,
        out_shape=(
            jax.ShapeDtypeStruct((rows, columns), jnp.float32),
            jax.ShapeDtypeStruct(small.shape, jnp.float32),
        ),
        in_specs=[vmem, vmem],
        out_specs=(vmem, vmem),
        scratch_shapes=[
            pltpu.VMEM(slot_shape, jnp.bfloat16),
            pltpu.VMEM(slot_shape, jnp.bfloat16),
            pltpu.VMEM((RING,) + small.shape, jnp.float32),
            pltpu.SemaphoreType.DMA(slot_shape[:3]),
            pltpu.SemaphoreType.DMA(slot_shape[:3]),
            pltpu.SemaphoreType.DMA((RING - 1,)),
            pltpu.SemaphoreType.DMA((RING - 1,)),
        ],
        compiler_params=pltpu.CompilerParams(collective_id=1, has_side_effects=True),
    )(grads, small)


PARTS = 4


def reduce_kernel(part_ref, sum_ref, near, chip_sum, far, total, send_sem, recv_sem):
    me = lax.axis_index("tensor")
    core = me % 2
    partner = me + 1 - 2 * core
    across = (me + 2) % 4
    half = part_ref.shape[0] // 2
    size = half // PARTS
    greet("tensor", (partner, across))

    def rows_of(side, piece):
        return pl.ds(pl.multiple_of(side * half + piece * size, size), size)

    def send(source, target, stage, piece, device):
        copy = pltpu.make_async_remote_copy(
            src_ref=source,
            dst_ref=target,
            send_sem=send_sem.at[stage, piece],
            recv_sem=recv_sem.at[stage, piece],
            device_id={"tensor": device},
            device_id_type=MESH,
        )
        copy.start()
        return copy

    first = [
        send(part_ref.at[rows_of(1 - core, piece)], near.at[piece], 0, piece, partner)
        for piece in range(PARTS)
    ]
    second = []
    for piece in range(PARTS):
        first[piece].wait_recv()
        chip = near[piece].astype(jnp.float32) + part_ref[rows_of(core, piece)].astype(jnp.float32)
        chip_sum[piece] = chip.astype(jnp.bfloat16)
        second.append(send(chip_sum.at[piece], far.at[piece], 1, piece, across))
    third = []
    for piece in range(PARTS):
        second[piece].wait_recv()
        both = chip_sum[piece].astype(jnp.float32) + far[piece].astype(jnp.float32)
        total[piece] = both.astype(jnp.bfloat16)
        third.append(send(total.at[piece], sum_ref.at[rows_of(core, piece)], 2, piece, partner))
    for piece in range(PARTS):
        third[piece].wait_recv()
        sum_ref[rows_of(core, piece)] = total[piece]
    for copy in first + second + third:
        copy.wait_send()


def tensor_sum(part, call):
    part = part.astype(jnp.bfloat16)
    if lax.axis_size("tensor") != 4 or part.shape[0] % 128:
        return lax.psum(part, "tensor").astype(jnp.float32)
    rows, columns = part.shape
    slots = pltpu.VMEM((PARTS, rows // (2 * PARTS), columns), jnp.bfloat16)
    vmem = pl.BlockSpec(memory_space=pltpu.VMEM)
    return pl.pallas_call(
        reduce_kernel,
        out_shape=jax.ShapeDtypeStruct(part.shape, jnp.bfloat16),
        in_specs=[vmem],
        out_specs=vmem,
        scratch_shapes=[
            slots,
            slots,
            slots,
            slots,
            pltpu.SemaphoreType.DMA((3, PARTS)),
            pltpu.SemaphoreType.DMA((3, PARTS)),
        ],
        compiler_params=pltpu.CompilerParams(collective_id=2 + call, has_side_effects=True),
    )(part).astype(jnp.float32)


def gather_weights(share):
    if lax.axis_size("dp") == RING and share.shape[0] % 32 == 0:
        return ring_gather(share)
    return lax.all_gather(share, "dp", axis=0, tiled=True)


def scatter_grads(grads, small):
    if lax.axis_size("dp") == RING and grads.shape[0] % (32 * RING) == 0:
        return ring_scatter(grads, small)
    share = lax.psum_scatter(grads, "dp", scatter_dimension=0, tiled=True)
    return share.astype(jnp.float32), lax.psum(small, "dp")


def matmul(left_op, right_op):
    return jnp.dot(left_op, right_op, preferred_element_type=jnp.float32)


def inner_rows(left_op, right_op):
    return lax.dot_general(
        left_op, right_op, (((0,), (0,)), ((), ())), preferred_element_type=jnp.float32
    )


def times_transposed(left_op, right_op):
    return lax.dot_general(
        left_op, right_op, (((1,), (1,)), ((), ())), preferred_element_type=jnp.float32
    )


def layer_norm(summed_rows, gain_vec, shift_vec):
    center = jnp.mean(summed_rows, -1, keepdims=True)
    offset = summed_rows - center
    inverse = lax.rsqrt(jnp.mean(offset * offset, -1, keepdims=True) + norm_eps)
    normed = offset * inverse
    return (normed * gain_vec + shift_vec, normed, inverse)


def norm_back(upstream, normed, inverse, gain_vec):
    scaled = upstream * gain_vec
    return inverse * (
        scaled
        - jnp.mean(scaled, -1, keepdims=True)
        - normed * jnp.mean(scaled * normed, -1, keepdims=True)
    )


def gelu_value(pre_act):
    return 0.5 * pre_act * (1.0 + jax.scipy.special.erf(pre_act * root_half))


def gelu_slope(pre_act):
    return (
        0.5 * (1.0 + jax.scipy.special.erf(pre_act * root_half))
        + pre_act * jnp.exp(-0.5 * pre_act * pre_act) * normal_peak
    )


def score_block(query_heads, key_heads, length):
    seq_len = query_heads.shape[0]
    scale_factor = query_heads.shape[-1] ** (-0.5)
    scores = (
        jnp.einsum("qhe,khe->hqk", query_heads, key_heads, preferred_element_type=jnp.float32)
        * scale_factor
    )
    usable = lax.broadcasted_iota(jnp.int32, (1, 1, seq_len), 2) < length
    return jnp.where(usable, scores, masked_score)


def attend_forward(operands):
    query_heads, key_heads, value_heads, length = operands
    scores = score_block(query_heads, key_heads, length)
    highest = jnp.max(scores, -1, keepdims=True)
    log_total = highest + jnp.log(jnp.sum(jnp.exp(scores - highest), -1, keepdims=True))
    probs_low = jnp.exp(scores - log_total).astype(jnp.bfloat16)
    mixed_heads = jnp.einsum(
        "hqk,khe->qhe", probs_low, value_heads, preferred_element_type=jnp.float32
    )
    return (mixed_heads.astype(jnp.bfloat16), log_total)


def attend_backward(operands):
    query_heads, key_heads, value_heads, grad_heads, log_total, length = operands
    scale_factor = query_heads.shape[-1] ** (-0.5)
    scores = score_block(query_heads, key_heads, length)
    probs = jnp.exp(scores - log_total)
    probs_low = probs.astype(jnp.bfloat16)
    grad_probs = jnp.einsum(
        "qhe,khe->hqk", grad_heads, value_heads, preferred_element_type=jnp.float32
    )
    row_dot = jnp.sum(probs * grad_probs, -1, keepdims=True)
    grad_scores = (probs * (grad_probs - row_dot) * scale_factor).astype(jnp.bfloat16)
    grad_query = jnp.einsum(
        "hqk,khe->qhe", grad_scores, key_heads, preferred_element_type=jnp.float32
    )
    grad_keys = jnp.einsum(
        "hqk,qhe->khe", grad_scores, query_heads, preferred_element_type=jnp.float32
    )
    grad_values = jnp.einsum(
        "hqk,qhe->khe", probs_low, grad_heads, preferred_element_type=jnp.float32
    )
    return (grad_query, grad_keys, grad_values)


def adam_update(param, grad, moments, decay):
    first = beta_first * moments[0] + (1.0 - beta_first) * grad
    second = beta_second * moments[1] + (1.0 - beta_second) * grad * grad
    first_hat = first / (1.0 - beta_first**step_count)
    second_hat = second / (1.0 - beta_second**step_count)
    new_param = param - learn_rate * (first_hat / (jnp.sqrt(second_hat) + adam_eps) + decay * param)
    return (new_param, jnp.stack([first, second]))


def local(
    tokens,
    cotangent,
    lengths,
    in_weight,
    out_weight,
    in_bias,
    norm_vec,
    in_moments,
    out_moments,
    bias_moments,
    norm_moments,
):
    seq_count, seq_len, width = tokens.shape
    row_count = seq_count * seq_len
    in_low = in_weight.astype(jnp.bfloat16)
    out_low = out_weight.astype(jnp.bfloat16).swapaxes(1, 2)
    share = jnp.concatenate(list(in_low[:3]) + [out_low[0]] + list(in_low[3:]) + list(out_low[1:]), 1)
    full = gather_weights(share)
    group_width = in_weight.shape[2]
    heads_here = group_width // HDIM
    w_qkv = full[:, : 3 * group_width]
    w_proj = full[:, 3 * group_width : 4 * group_width]
    w_up = full[:, 4 * group_width : 8 * group_width]
    w_down = full[:, 8 * group_width :]
    bias_up = in_bias[2:6].reshape(1, 4 * group_width)

    def split_heads(flat_rows):
        return flat_rows.reshape(seq_count, seq_len, heads_here, HDIM)

    flat_tokens = tokens.reshape(row_count, width)
    qkv = matmul(flat_tokens, w_qkv)
    query = (qkv[:, :group_width] + in_bias[0]).astype(jnp.bfloat16)
    keys_low = qkv[:, group_width : 2 * group_width].astype(jnp.bfloat16)
    values_low = (qkv[:, 2 * group_width :] + in_bias[1]).astype(jnp.bfloat16)
    mixed_heads, log_total = lax.map(
        attend_forward,
        (split_heads(query), split_heads(keys_low), split_heads(values_low), lengths),
    )
    mixed_flat = mixed_heads.reshape(row_count, group_width)
    attn_out = tensor_sum(times_transposed(mixed_flat, w_proj), 0)
    hidden, normed_one, inverse_one = layer_norm(
        flat_tokens.astype(jnp.float32) + attn_out + norm_vec[0], norm_vec[1], norm_vec[2]
    )
    hidden_low = hidden.astype(jnp.bfloat16)
    pre_act = matmul(hidden_low, w_up) + bias_up
    act_low = gelu_value(pre_act).astype(jnp.bfloat16)
    ffn_out = tensor_sum(times_transposed(act_low, w_down), 1)
    out_rows, normed_two, inverse_two = layer_norm(
        hidden + ffn_out + norm_vec[3], norm_vec[4], norm_vec[5]
    )
    positions = lax.broadcasted_iota(jnp.int32, (seq_count, seq_len), 1)
    live_rows = (positions < lengths[:, None]).astype(jnp.float32).reshape(row_count, 1)
    grad_out = cotangent.reshape(row_count, width).astype(jnp.float32) * live_rows
    grad_two = norm_back(grad_out, normed_two, inverse_two, norm_vec[4])
    grad_two_low = grad_two.astype(jnp.bfloat16)
    grad_down = inner_rows(grad_two_low, act_low).astype(jnp.bfloat16)
    grad_act = matmul(grad_two_low, w_down)
    grad_pre = grad_act * gelu_slope(pre_act)
    grad_pre_low = grad_pre.astype(jnp.bfloat16)
    grad_up = inner_rows(hidden_low, grad_pre_low).astype(jnp.bfloat16)
    grad_hidden = grad_two + tensor_sum(times_transposed(grad_pre_low, w_up), 2)
    grad_one = norm_back(grad_hidden, normed_one, inverse_one, norm_vec[1])
    grad_one_low = grad_one.astype(jnp.bfloat16)
    grad_proj = inner_rows(grad_one_low, mixed_flat).astype(jnp.bfloat16)
    grad_mixed = matmul(grad_one_low, w_proj).astype(jnp.bfloat16)
    grad_query, grad_keys, grad_values = lax.map(
        attend_backward,
        (
            split_heads(query),
            split_heads(keys_low),
            split_heads(values_low),
            split_heads(grad_mixed),
            log_total,
            lengths,
        ),
    )
    grad_query = grad_query.reshape(row_count, group_width)
    grad_keys = grad_keys.reshape(row_count, group_width)
    grad_values = grad_values.reshape(row_count, group_width)
    qkv_grad_low = jnp.concatenate([grad_query, grad_keys, grad_values], 1).astype(jnp.bfloat16)
    grad_input = grad_one + tensor_sum(times_transposed(qkv_grad_low, w_qkv), 3)
    grad_qkv = inner_rows(flat_tokens, qkv_grad_low).astype(jnp.bfloat16)
    grads = jnp.concatenate([grad_qkv, grad_proj, grad_up, grad_down], 1)
    bias_rows = jnp.concatenate(
        [jnp.sum(grad_query, 0), jnp.sum(grad_values, 0), jnp.sum(grad_pre, 0)]
    ).reshape(6, group_width)
    norm_rows = jnp.stack(
        [
            jnp.sum(grad_one, 0),
            jnp.sum(grad_hidden * normed_one, 0),
            jnp.sum(grad_hidden, 0),
            jnp.sum(grad_two, 0),
            jnp.sum(grad_out * normed_two, 0),
            jnp.sum(grad_out, 0),
        ]
    )
    small = jnp.pad(jnp.concatenate([norm_rows, bias_rows], 1), ((0, 2), (0, 64)))
    share_total, small_total = scatter_grads(grads, small)
    norm_total = small_total[:6, :width]
    bias_total = small_total[:6, width : width + group_width]
    blocks = [share_total[:, k * group_width : (k + 1) * group_width] for k in range(12)]
    in_share = jnp.stack(blocks[:3] + blocks[4:8])
    out_share = jnp.stack([blocks[3]] + blocks[8:]).swapaxes(1, 2)
    new_in_weight, new_in_moments = adam_update(in_weight, in_share, in_moments, weight_decay)
    new_out_weight, new_out_moments = adam_update(out_weight, out_share, out_moments, weight_decay)
    new_in_bias, new_bias_moments = adam_update(in_bias, bias_total, bias_moments, 0.0)
    new_norm_vec, new_norm_moments = adam_update(norm_vec, norm_total, norm_moments, 0.0)
    output = out_rows.astype(jnp.bfloat16).reshape(seq_count, seq_len, width)
    grad_tokens = grad_input.astype(jnp.bfloat16).reshape(seq_count, seq_len, width)
    return (
        output,
        grad_tokens,
        in_share,
        out_share,
        bias_total,
        norm_total,
        new_in_weight,
        new_out_weight,
        new_in_bias,
        new_norm_vec,
        new_in_moments,
        new_out_moments,
        new_bias_moments,
        new_norm_moments,
    )


def solution(mesh):
    in_specs = (
        P("dp", None, None),
        P("dp", None, None),
        P("dp"),
        P(None, "dp", "tensor"),
        P(None, "tensor", "dp"),
        P(None, "tensor"),
        P(),
        P(None, None, "dp", "tensor"),
        P(None, None, "tensor", "dp"),
        P(None, None, "tensor"),
        P(),
    )
    out_specs = (
        P("dp", None, None),
        P("dp", None, None),
        P(None, "dp", "tensor"),
        P(None, "tensor", "dp"),
        P(None, "tensor"),
        P(),
        P(None, "dp", "tensor"),
        P(None, "tensor", "dp"),
        P(None, "tensor"),
        P(),
        P(None, None, "dp", "tensor"),
        P(None, None, "tensor", "dp"),
        P(None, None, "tensor"),
        P(),
    )
    return jax.shard_map(local, mesh=mesh, in_specs=in_specs, out_specs=out_specs, check_vma=False)
```

```python
import jax
import jax.numpy as jnp
from jax import lax
from jax.experimental import pallas as pl
from jax.experimental.pallas import tpu as pltpu
from jax.sharding import PartitionSpec as P

HDIM = 64


norm_eps = 1e-12
masked_score = -1e30
learn_rate = 0.005
beta_first = 0.9
beta_second = 0.999
adam_eps = 1e-08
weight_decay = 0.01
step_count = 2.0
root_half = 0.7071067811865476
normal_peak = 0.3989422804014327


RING = 8
MESH = pl.DeviceIdType.MESH


def ring_place(index):
    depth, side = index // 2, index % 2
    return depth + side * (RING - 1 - 2 * depth)


def ring_device(place):
    side = place // (RING // 2)
    depth = place + side * (RING - 1 - 2 * place)
    return 2 * depth + side


def ring_neighbours():
    me = lax.axis_index("dp")
    place = ring_place(me)
    right = ring_device((place + 1) % RING)
    left = ring_device((place + RING - 1) % RING)
    return me, place, (right, left)


PIECES = 2
PARTS = 4


def gather_steps(share_ref, full_ref, local_sem, send_sem, recv_sem):
    me, place, targets = ring_neighbours()
    rows, columns = share_ref.shape
    piece_rows, half = rows // PIECES, columns // 2

    def full_at(owner, piece, way):
        start = pl.multiple_of(owner * rows + piece * piece_rows, piece_rows)
        return full_ref.at[pl.ds(start, piece_rows), pl.ds(way * half, half)]

    own_start = pl.multiple_of(me * rows, rows)
    own = pltpu.make_async_copy(share_ref, full_ref.at[pl.ds(own_start, rows)], local_sem)
    own.start()
    copies = {}
    for step in range(RING - 1):
        for piece in range(PIECES):
            for way in range(2):
                if step:
                    copies[step - 1, piece, way].wait_recv()
                shift = RING - step if way == 0 else step
                owner = ring_device((place + shift) % RING)
                target = full_at(owner, piece, way)
                source = target
                if step == 0:
                    source = share_ref.at[
                        pl.ds(piece * piece_rows, piece_rows), pl.ds(way * half, half)
                    ]
                copy = pltpu.make_async_remote_copy(
                    src_ref=source,
                    dst_ref=target,
                    send_sem=send_sem.at[step, piece, way],
                    recv_sem=recv_sem.at[step, piece, way],
                    device_id={"dp": targets[way]},
                    device_id_type=MESH,
                )
                copy.start()
                copies[step, piece, way] = copy
        yield
    for (step, piece, way), copy in copies.items():
        copy.wait_send()
        if step == RING - 2:
            copy.wait_recv()
    own.wait()


def scatter_steps(grad_ref, share_ref, arrived, leaving, send_sem, recv_sem):
    me, place, targets = ring_neighbours()
    rows, columns = share_ref.shape
    piece_rows, half = rows // PIECES, columns // 2

    def grad_at(owner, piece, way):
        start = pl.multiple_of(owner * rows + piece * piece_rows, piece_rows)
        return grad_ref.at[pl.ds(start, piece_rows), pl.ds(way * half, half)]

    copies = {}
    for step in range(RING - 1):
        for piece in range(PIECES):
            for way in range(2):
                shift = RING - 1 - step if way == 0 else 1 + step
                source = grad_at(ring_device((place + shift) % RING), piece, way)
                if step:
                    copies[step - 1, piece, way].wait_recv()
                    running = arrived[step - 1, piece, way].astype(jnp.float32)
                    running += source[...].astype(jnp.float32)
                    leaving[step, piece, way] = running.astype(jnp.bfloat16)
                    source = leaving.at[step, piece, way]
                copy = pltpu.make_async_remote_copy(
                    src_ref=source,
                    dst_ref=arrived.at[step, piece, way],
                    send_sem=send_sem.at[step, piece, way],
                    recv_sem=recv_sem.at[step, piece, way],
                    device_id={"dp": targets[way]},
                    device_id_type=MESH,
                )
                copy.start()
                copies[step, piece, way] = copy
        yield
    for piece in range(PIECES):
        for way in range(2):
            copies[RING - 2, piece, way].wait_recv()
            total = arrived[RING - 2, piece, way].astype(jnp.float32)
            total += grad_at(me, piece, way)[...].astype(jnp.float32)
            share_ref[pl.ds(piece * piece_rows, piece_rows), pl.ds(way * half, half)] = total
    for copy in copies.values():
        copy.wait_send()


def small_steps(small_ref, small_out_ref, small_slots, small_send, small_recv):
    me = lax.axis_index("dp")
    small_copies = []
    for shift in range(1, RING):
        copy = pltpu.make_async_remote_copy(
            src_ref=small_ref,
            dst_ref=small_slots.at[me],
            send_sem=small_send.at[shift - 1],
            recv_sem=small_recv.at[shift - 1],
            device_id={"dp": (me + shift) % RING},
            device_id_type=MESH,
        )
        copy.start()
        small_copies.append(copy)
    for turn in range(4):
        yield
    for copy in small_copies:
        copy.wait_recv()
    small_slots[me] = small_ref[...]
    small_total = small_slots[0]
    for index in range(1, RING):
        small_total += small_slots[index]
    small_out_ref[...] = small_total
    for copy in small_copies:
        copy.wait_send()


def tensor_partners():
    me = lax.axis_index("tensor")
    return me + 1 - 2 * (me % 2), (me + 2) % 4


def sum_steps(part_ref, sum_ref, near, chip_sum, far, total, send_sem, recv_sem):
    core = lax.axis_index("tensor") % 2
    partner, across = tensor_partners()
    half = part_ref.shape[0] // 2
    size = half // PARTS

    def rows_of(side, piece):
        return pl.ds(pl.multiple_of(side * half + piece * size, size), size)

    def send(source, target, stage, piece, device):
        copy = pltpu.make_async_remote_copy(
            src_ref=source,
            dst_ref=target,
            send_sem=send_sem.at[stage, piece],
            recv_sem=recv_sem.at[stage, piece],
            device_id={"tensor": device},
            device_id_type=MESH,
        )
        copy.start()
        return copy

    first = [
        send(part_ref.at[rows_of(1 - core, piece)], near.at[piece], 0, piece, partner)
        for piece in range(PARTS)
    ]
    second = []
    for piece in range(PARTS):
        first[piece].wait_recv()
        chip = near[piece].astype(jnp.float32) + part_ref[rows_of(core, piece)].astype(jnp.float32)
        chip_sum[piece] = chip.astype(jnp.bfloat16)
        second.append(send(chip_sum.at[piece], far.at[piece], 1, piece, across))
    yield
    third = []
    for piece in range(PARTS):
        second[piece].wait_recv()
        both = chip_sum[piece].astype(jnp.float32) + far[piece].astype(jnp.float32)
        total[piece] = both.astype(jnp.bfloat16)
        third.append(send(total.at[piece], sum_ref.at[rows_of(core, piece)], 2, piece, partner))
        if piece % 2:
            yield
    for piece in range(PARTS):
        third[piece].wait_recv()
        sum_ref[rows_of(core, piece)] = total[piece]
    for copy in first + second + third:
        copy.wait_send()


def take_turns(*plans):
    plans = list(plans)
    while plans:
        for plan in list(plans):
            if next(plan, "done") == "done":
                plans.remove(plan)


def greet_all(ring=(), tensor=()):
    barrier = pltpu.get_barrier_semaphore()
    for axis, devices in (("dp", ring), ("tensor", tensor)):
        for device in devices:
            pl.semaphore_signal(barrier, inc=1, device_id={axis: device}, device_id_type=MESH)
    pl.semaphore_wait(barrier, len(ring) + len(tensor))


def first_gather_kernel(in_ref, out_ref, full_ref, rest_ref, wide, share, *sems):
    width = in_ref.shape[2]
    for index in range(12):
        if index == 3 or index >= 8:
            block = out_ref[0 if index == 3 else index - 7].T
        else:
            block = in_ref[index if index < 3 else index - 1]
        wide[:, index * width : (index + 1) * width] = block
    share[...] = wide[:, : 4 * width].astype(jnp.bfloat16)
    rest_ref[...] = wide[:, 4 * width :].astype(jnp.bfloat16)
    greet_all(ring_neighbours()[2])
    take_turns(gather_steps(share, full_ref, *sems))


def second_gather_kernel(share_ref, part_ref, full_ref, sum_ref, *scratch):
    greet_all(ring_neighbours()[2], tensor_partners())
    take_turns(
        gather_steps(share_ref, full_ref, *scratch[:3]), sum_steps(part_ref, sum_ref, *scratch[3:])
    )


def sum_kernel(part_ref, sum_ref, *scratch):
    greet_all((), tensor_partners())
    take_turns(sum_steps(part_ref, sum_ref, *scratch))


def first_scatter_kernel(grad_ref, part_ref, share_ref, sum_ref, *scratch):
    greet_all(ring_neighbours()[2], tensor_partners())
    take_turns(
        scatter_steps(grad_ref, share_ref, *scratch[:4]),
        sum_steps(part_ref, sum_ref, *scratch[4:]),
    )


def second_scatter_kernel(
    grad_ref, part_ref, small_ref, share_ref, sum_ref, small_out_ref, *scratch
):
    me = lax.axis_index("dp")
    greet_all([(me + shift) % RING for shift in range(1, RING)], tensor_partners())
    take_turns(
        scatter_steps(grad_ref, share_ref, *scratch[:4]),
        sum_steps(part_ref, sum_ref, *scratch[4:10]),
        small_steps(small_ref, small_out_ref, *scratch[10:]),
    )


def gather_scratch():
    shape = (RING - 1, PIECES, 2)
    return [pltpu.SemaphoreType.DMA, pltpu.SemaphoreType.DMA(shape), pltpu.SemaphoreType.DMA(shape)]


def scatter_scratch(rows, columns):
    shape = (RING - 1, PIECES, 2)
    slots = pltpu.VMEM(shape + (rows // PIECES, columns // 2), jnp.bfloat16)
    return [slots, slots, pltpu.SemaphoreType.DMA(shape), pltpu.SemaphoreType.DMA(shape)]


def small_scratch(small):
    sems = pltpu.SemaphoreType.DMA((RING - 1,))
    return [pltpu.VMEM((RING,) + small.shape, jnp.float32), sems, sems]


def sum_scratch(rows, columns):
    slots = pltpu.VMEM((PARTS, rows // (2 * PARTS), columns), jnp.bfloat16)
    sems = pltpu.SemaphoreType.DMA((3, PARTS))
    return [slots, slots, slots, slots, sems, sems]


def kernel_call(kernel, operands, results, scratch, collective_id):
    vmem = pl.BlockSpec(memory_space=pltpu.VMEM)
    extra = {} if collective_id is None else {"collective_id": collective_id, "has_side_effects": True}
    return pl.pallas_call(
        kernel,
        out_shape=tuple(jax.ShapeDtypeStruct(shape, dtype) for shape, dtype in results),
        in_specs=[vmem] * len(operands),
        out_specs=(vmem,) * len(results),
        scratch_shapes=scratch,
        compiler_params=pltpu.CompilerParams(**extra),
    )(*operands)


def ring_here(rows):
    return (
        lax.axis_size("dp") == RING
        and lax.axis_size("tensor") == 4
        and rows % 32 == 0
    )


def gather_first(in_weight, out_weight):
    rows, group_width = in_weight.shape[1:]
    if ring_here(rows):
        return kernel_call(
            first_gather_kernel,
            (in_weight, out_weight),
            [
                ((RING * rows, 4 * group_width), jnp.bfloat16),
                ((rows, 8 * group_width), jnp.bfloat16),
            ],
            [
                pltpu.VMEM((rows, 12 * group_width), jnp.float32),
                pltpu.VMEM((rows, 4 * group_width), jnp.bfloat16),
            ]
            + gather_scratch(),
            0,
        )
    in_low = in_weight.astype(jnp.bfloat16)
    out_low = out_weight.astype(jnp.bfloat16).swapaxes(1, 2)
    share = jnp.concatenate(list(in_low[:3]) + [out_low[0]], 1)
    rest = jnp.concatenate(list(in_low[3:]) + list(out_low[1:]), 1)
    return lax.all_gather(share, "dp", axis=0, tiled=True), rest


def plain_sum(part):
    if lax.axis_size("tensor") == 4 and part.shape[0] % 128 == 0:
        results = [(part.shape, jnp.bfloat16)]
        return kernel_call(sum_kernel, (part,), results, sum_scratch(*part.shape), 1)[0]
    return lax.psum(part, "tensor")


def gather_second(rest, part):
    rows, columns = rest.shape
    if ring_here(rows):
        return kernel_call(
            second_gather_kernel,
            (rest, part),
            [((RING * rows, columns), jnp.bfloat16), (part.shape, jnp.bfloat16)],
            gather_scratch() + sum_scratch(*part.shape),
            2,
        )
    return lax.all_gather(rest, "dp", axis=0, tiled=True), lax.psum(part, "tensor")


def scatter_plain(grads):
    share = lax.psum_scatter(grads, "dp", scatter_dimension=0, tiled=True)
    return share.astype(jnp.float32)


def scatter_first(grads, part):
    rows, columns = grads.shape[0] // lax.axis_size("dp"), grads.shape[1]
    if ring_here(rows):
        return kernel_call(
            first_scatter_kernel,
            (grads, part),
            [((rows, columns), jnp.float32), (part.shape, jnp.bfloat16)],
            scatter_scratch(rows, columns) + sum_scratch(*part.shape),
            3,
        )
    return scatter_plain(grads), lax.psum(part, "tensor")


def scatter_second(grads, part, small):
    rows, columns = grads.shape[0] // lax.axis_size("dp"), grads.shape[1]
    if ring_here(rows):
        return kernel_call(
            second_scatter_kernel,
            (grads, part, small),
            [
                ((rows, columns), jnp.float32),
                (part.shape, jnp.bfloat16),
                (small.shape, jnp.float32),
            ],
            scatter_scratch(rows, columns) + sum_scratch(*part.shape) + small_scratch(small),
            4,
        )
    return scatter_plain(grads), lax.psum(part, "tensor"), lax.psum(small, "dp")


def matmul(left_op, right_op):
    return jnp.dot(left_op, right_op, preferred_element_type=jnp.float32)


def inner_rows(left_op, right_op):
    return lax.dot_general(
        left_op, right_op, (((0,), (0,)), ((), ())), preferred_element_type=jnp.float32
    )


def times_transposed(left_op, right_op):
    return lax.dot_general(
        left_op, right_op, (((1,), (1,)), ((), ())), preferred_element_type=jnp.float32
    )


def layer_norm(summed_rows, gain_vec, shift_vec):
    center = jnp.mean(summed_rows, -1, keepdims=True)
    offset = summed_rows - center
    inverse = lax.rsqrt(jnp.mean(offset * offset, -1, keepdims=True) + norm_eps)
    normed = offset * inverse
    return (normed * gain_vec + shift_vec, normed, inverse)


def norm_back(upstream, normed, inverse, gain_vec):
    scaled = upstream * gain_vec
    return inverse * (
        scaled
        - jnp.mean(scaled, -1, keepdims=True)
        - normed * jnp.mean(scaled * normed, -1, keepdims=True)
    )


def gelu_value(pre_act):
    return 0.5 * pre_act * (1.0 + jax.scipy.special.erf(pre_act * root_half))


def gelu_slope(pre_act):
    return (
        0.5 * (1.0 + jax.scipy.special.erf(pre_act * root_half))
        + pre_act * jnp.exp(-0.5 * pre_act * pre_act) * normal_peak
    )


def score_block(query_heads, key_heads, length):
    seq_len = query_heads.shape[0]
    scale_factor = query_heads.shape[-1] ** (-0.5)
    scores = (
        jnp.einsum("qhe,khe->hqk", query_heads, key_heads, preferred_element_type=jnp.float32)
        * scale_factor
    )
    usable = lax.broadcasted_iota(jnp.int32, (1, 1, seq_len), 2) < length
    return jnp.where(usable, scores, masked_score)


def attend_forward(operands):
    query_heads, key_heads, value_heads, length = operands
    scores = score_block(query_heads, key_heads, length)
    highest = jnp.max(scores, -1, keepdims=True)
    log_total = highest + jnp.log(jnp.sum(jnp.exp(scores - highest), -1, keepdims=True))
    probs_low = jnp.exp(scores - log_total).astype(jnp.bfloat16)
    mixed_heads = jnp.einsum(
        "hqk,khe->qhe", probs_low, value_heads, preferred_element_type=jnp.float32
    )
    return (mixed_heads.astype(jnp.bfloat16), log_total)


def attend_backward(operands):
    query_heads, key_heads, value_heads, grad_heads, log_total, length = operands
    scale_factor = query_heads.shape[-1] ** (-0.5)
    scores = score_block(query_heads, key_heads, length)
    probs = jnp.exp(scores - log_total)
    probs_low = probs.astype(jnp.bfloat16)
    grad_probs = jnp.einsum(
        "qhe,khe->hqk", grad_heads, value_heads, preferred_element_type=jnp.float32
    )
    row_dot = jnp.sum(probs * grad_probs, -1, keepdims=True)
    grad_scores = (probs * (grad_probs - row_dot) * scale_factor).astype(jnp.bfloat16)
    grad_query = jnp.einsum(
        "hqk,khe->qhe", grad_scores, key_heads, preferred_element_type=jnp.float32
    )
    grad_keys = jnp.einsum(
        "hqk,qhe->khe", grad_scores, query_heads, preferred_element_type=jnp.float32
    )
    grad_values = jnp.einsum(
        "hqk,qhe->khe", probs_low, grad_heads, preferred_element_type=jnp.float32
    )
    return (grad_query, grad_keys, grad_values)


def adam_update(param, grad, moments, decay):
    first = beta_first * moments[0] + (1.0 - beta_first) * grad
    second = beta_second * moments[1] + (1.0 - beta_second) * grad * grad
    first_hat = first / (1.0 - beta_first**step_count)
    second_hat = second / (1.0 - beta_second**step_count)
    new_param = param - learn_rate * (first_hat / (jnp.sqrt(second_hat) + adam_eps) + decay * param)
    return (new_param, jnp.stack([first, second]))


def adam_store(param, grad, moments, decay, new_param, new_moments):
    first = beta_first * moments[0] + (1.0 - beta_first) * grad
    second = beta_second * moments[1] + (1.0 - beta_second) * grad * grad
    first_hat = first / (1.0 - beta_first**step_count)
    second_hat = second / (1.0 - beta_second**step_count)
    step = first_hat / (jnp.sqrt(second_hat) + adam_eps) + decay * param
    new_param[...] = param - learn_rate * step
    new_moments[0] = first
    new_moments[1] = second


def adam_kernel(share_ref, rest_ref, small_ref, *refs):
    params, moments = refs[:4], refs[4:8]
    grads, new_params, new_moments = refs[8:12], refs[12:16], refs[16:20]
    matrix_in, matrix_out = params[0], params[1]
    width = matrix_in.shape[2]
    for index in range(12):
        source, place = (share_ref, index) if index < 4 else (rest_ref, index - 4)
        grad = source[:, place * width : (place + 1) * width]
        if index == 3 or index >= 8:
            group, spot, grad = 1, (0 if index == 3 else index - 7), grad.T
        else:
            group, spot = 0, (index if index < 3 else index - 1)
        grads[group][spot] = grad
        adam_store(
            params[group][spot],
            grad,
            (moments[group][0, spot], moments[group][1, spot]),
            weight_decay,
            new_params[group].at[spot],
            new_moments[group].at[:, spot],
        )
    model_width = params[3].shape[1]
    for group, start in ((2, model_width), (3, 0)):
        grad = small_ref[:6, start : start + params[group].shape[1]]
        grads[group][...] = grad
        adam_store(
            params[group][...], grad, moments[group], 0.0, new_params[group], new_moments[group]
        )


def update_all(share, rest, small, params, moments):
    group_width, width = params[0].shape[2], params[3].shape[1]
    if ring_here(params[0].shape[1]):
        shapes = [(a.shape, jnp.float32) for a in params + params + moments]
        return kernel_call(adam_kernel, (share, rest, small) + params + moments, shapes, [], None)
    total = jnp.concatenate([share, rest], 1)
    blocks = [total[:, k * group_width : (k + 1) * group_width] for k in range(12)]
    grads = (
        jnp.stack(blocks[:3] + blocks[4:8]),
        jnp.stack([blocks[3]] + blocks[8:]).swapaxes(1, 2),
        small[:6, width : width + group_width],
        small[:6, :width],
    )
    decays = (weight_decay, weight_decay, 0.0, 0.0)
    news = [adam_update(*group) for group in zip(params, grads, moments, decays)]
    return grads + tuple(n[0] for n in news) + tuple(n[1] for n in news)


def local(
    tokens,
    cotangent,
    lengths,
    in_weight,
    out_weight,
    in_bias,
    norm_vec,
    in_moments,
    out_moments,
    bias_moments,
    norm_moments,
):
    seq_count, seq_len, width = tokens.shape
    row_count = seq_count * seq_len
    first_full, rest = gather_first(in_weight, out_weight)
    group_width = in_weight.shape[2]
    heads_here = group_width // HDIM
    w_qkv = first_full[:, : 3 * group_width]
    w_proj = first_full[:, 3 * group_width :]
    bias_up = in_bias[2:6].reshape(1, 4 * group_width)

    def split_heads(flat_rows):
        return flat_rows.reshape(seq_count, seq_len, heads_here, HDIM)

    flat_tokens = tokens.reshape(row_count, width)
    qkv = matmul(flat_tokens, w_qkv)
    query = (qkv[:, :group_width] + in_bias[0]).astype(jnp.bfloat16)
    keys_low = qkv[:, group_width : 2 * group_width].astype(jnp.bfloat16)
    values_low = (qkv[:, 2 * group_width :] + in_bias[1]).astype(jnp.bfloat16)
    mixed_heads, log_total = lax.map(
        attend_forward,
        (split_heads(query), split_heads(keys_low), split_heads(values_low), lengths),
    )
    mixed_flat = mixed_heads.reshape(row_count, group_width)
    attn_part = times_transposed(mixed_flat, w_proj).astype(jnp.bfloat16)
    second_full, attn_out = gather_second(rest, attn_part)
    w_up = second_full[:, : 4 * group_width]
    w_down = second_full[:, 4 * group_width :]
    hidden, normed_one, inverse_one = layer_norm(
        flat_tokens.astype(jnp.float32) + attn_out.astype(jnp.float32) + norm_vec[0], norm_vec[1], norm_vec[2]
    )
    hidden_low = hidden.astype(jnp.bfloat16)
    pre_act = matmul(hidden_low, w_up) + bias_up
    act_low = gelu_value(pre_act).astype(jnp.bfloat16)
    ffn_part = times_transposed(act_low, w_down).astype(jnp.bfloat16)
    ffn_out = plain_sum(ffn_part).astype(jnp.float32)
    out_rows, normed_two, inverse_two = layer_norm(
        hidden + ffn_out + norm_vec[3], norm_vec[4], norm_vec[5]
    )
    positions = lax.broadcasted_iota(jnp.int32, (seq_count, seq_len), 1)
    live_rows = (positions < lengths[:, None]).astype(jnp.float32).reshape(row_count, 1)
    grad_out = cotangent.reshape(row_count, width).astype(jnp.float32) * live_rows
    grad_two = norm_back(grad_out, normed_two, inverse_two, norm_vec[4])
    grad_two_low = grad_two.astype(jnp.bfloat16)
    grad_down = inner_rows(grad_two_low, act_low).astype(jnp.bfloat16)
    grad_act = matmul(grad_two_low, w_down)
    grad_pre = grad_act * gelu_slope(pre_act)
    grad_pre_low = grad_pre.astype(jnp.bfloat16)
    grad_up = inner_rows(hidden_low, grad_pre_low).astype(jnp.bfloat16)
    rest_grads = jnp.concatenate([grad_up, grad_down], 1)
    back_part = times_transposed(grad_pre_low, w_up).astype(jnp.bfloat16)
    rest_total, back_sum = scatter_first(rest_grads, back_part)
    grad_hidden = grad_two + back_sum.astype(jnp.float32)
    grad_one = norm_back(grad_hidden, normed_one, inverse_one, norm_vec[1])
    grad_one_low = grad_one.astype(jnp.bfloat16)
    grad_proj = inner_rows(grad_one_low, mixed_flat).astype(jnp.bfloat16)
    grad_mixed = matmul(grad_one_low, w_proj).astype(jnp.bfloat16)
    grad_query, grad_keys, grad_values = lax.map(
        attend_backward,
        (
            split_heads(query),
            split_heads(keys_low),
            split_heads(values_low),
            split_heads(grad_mixed),
            log_total,
            lengths,
        ),
    )
    grad_query = grad_query.reshape(row_count, group_width)
    grad_keys = grad_keys.reshape(row_count, group_width)
    grad_values = grad_values.reshape(row_count, group_width)
    qkv_grad_low = jnp.concatenate([grad_query, grad_keys, grad_values], 1).astype(jnp.bfloat16)
    input_part = times_transposed(qkv_grad_low, w_qkv).astype(jnp.bfloat16)
    grad_qkv = inner_rows(flat_tokens, qkv_grad_low).astype(jnp.bfloat16)
    first_grads = jnp.concatenate([grad_qkv, grad_proj], 1)
    bias_rows = jnp.concatenate(
        [jnp.sum(grad_query, 0), jnp.sum(grad_values, 0), jnp.sum(grad_pre, 0)]
    ).reshape(6, group_width)
    norm_rows = jnp.stack(
        [
            jnp.sum(grad_one, 0),
            jnp.sum(grad_hidden * normed_one, 0),
            jnp.sum(grad_hidden, 0),
            jnp.sum(grad_two, 0),
            jnp.sum(grad_out * normed_two, 0),
            jnp.sum(grad_out, 0),
        ]
    )
    small = jnp.pad(jnp.concatenate([norm_rows, bias_rows], 1), ((0, 2), (0, 64)))
    share_total, input_sum, small_total = scatter_second(first_grads, input_part, small)
    grad_input = grad_one + input_sum.astype(jnp.float32)
    params = (in_weight, out_weight, in_bias, norm_vec)
    moments = (in_moments, out_moments, bias_moments, norm_moments)
    updates = update_all(share_total, rest_total, small_total, params, moments)
    output = out_rows.astype(jnp.bfloat16).reshape(seq_count, seq_len, width)
    grad_tokens = grad_input.astype(jnp.bfloat16).reshape(seq_count, seq_len, width)
    return (
        output,
        grad_tokens,
    ) + tuple(updates)


def solution(mesh):
    in_specs = (
        P("dp", None, None),
        P("dp", None, None),
        P("dp"),
        P(None, "dp", "tensor"),
        P(None, "tensor", "dp"),
        P(None, "tensor"),
        P(),
        P(None, None, "dp", "tensor"),
        P(None, None, "tensor", "dp"),
        P(None, None, "tensor"),
        P(),
    )
    out_specs = (
        P("dp", None, None),
        P("dp", None, None),
        P(None, "dp", "tensor"),
        P(None, "tensor", "dp"),
        P(None, "tensor"),
        P(),
        P(None, "dp", "tensor"),
        P(None, "tensor", "dp"),
        P(None, "tensor"),
        P(),
        P(None, None, "dp", "tensor"),
        P(None, None, "tensor", "dp"),
        P(None, None, "tensor"),
        P(),
    )
    return jax.shard_map(local, mesh=mesh, in_specs=in_specs, out_specs=out_specs, check_vma=False)
```

```python
import jax
import jax.numpy as jnp
from jax import lax
from jax.experimental import pallas as pl
from jax.experimental.pallas import tpu as pltpu
from jax.sharding import PartitionSpec as P

HDIM = 64


norm_eps = 1e-12
masked_score = -1e30
learn_rate = 0.005
beta_first = 0.9
beta_second = 0.999
adam_eps = 1e-08
weight_decay = 0.01
step_count = 2.0
root_half = 0.7071067811865476
normal_peak = 0.3989422804014327


RING = 8
MESH = pl.DeviceIdType.MESH


def ring_place(index):
    depth, side = index // 2, index % 2
    return depth + side * (RING - 1 - 2 * depth)


def ring_device(place):
    side = place // (RING // 2)
    depth = place + side * (RING - 1 - 2 * place)
    return 2 * depth + side


def ring_neighbours():
    me = lax.axis_index("dp")
    place = ring_place(me)
    right = ring_device((place + 1) % RING)
    left = ring_device((place + RING - 1) % RING)
    return me, place, (right, left)


PIECES = 2
GATHER_SPLIT = 3
SCATTER_SPLIT = 4
PARTS = 4


def gather_steps(
    share_ref, full_ref, local_sem, send_sem, recv_sem, first=0, last=RING - 1, pace=1
):
    me, place, targets = ring_neighbours()
    rows, half = full_ref.shape[0] // RING, full_ref.shape[1] // 2
    piece_rows = rows // PIECES

    def block(ref, owner, piece, way):
        start = pl.multiple_of(owner * rows + piece * piece_rows, piece_rows)
        return ref.at[pl.ds(start, piece_rows), pl.ds(way * half, half)]

    def owner_of(step, way):
        return ring_device((place + (RING - step if way == 0 else step)) % RING)

    held = []
    if first == 0:
        own_start = pl.multiple_of(me * rows, rows)
        target = full_ref.at[pl.ds(own_start, rows)]
        held.append(pltpu.make_async_copy(share_ref, target, local_sem.at[0]))
    else:
        for step in range(first + 1):
            for way in range(2):
                start = pl.multiple_of(owner_of(step, way) * rows, rows)
                spot = (pl.ds(start, rows), pl.ds(way * half, half))
                sem = local_sem.at[2 * step + way]
                held.append(pltpu.make_async_copy(share_ref.at[spot], full_ref.at[spot], sem))
    copies = {}
    for step in range(first, last):
        for piece in range(PIECES):
            for way in range(2):
                owner = owner_of(step, way)
                target = source = block(full_ref, owner, piece, way)
                if step > first:
                    copies[step - 1, piece, way].wait_recv()
                elif step == 0:
                    source = share_ref.at[
                        pl.ds(piece * piece_rows, piece_rows), pl.ds(way * half, half)
                    ]
                else:
                    source = block(share_ref, owner, piece, way)
                copy = pltpu.make_async_remote_copy(
                    src_ref=source,
                    dst_ref=target,
                    send_sem=send_sem.at[step, piece, way],
                    recv_sem=recv_sem.at[step, piece, way],
                    device_id={"dp": targets[way]},
                    device_id_type=MESH,
                )
                copy.start()
                copies[step, piece, way] = copy
        if step == first:
            for copy in held:
                copy.start()
        for turn in range(pace):
            yield
    for (step, piece, way), copy in copies.items():
        copy.wait_send()
        if step == last - 1:
            copy.wait_recv()
    for copy in held:
        copy.wait()


def scatter_steps(
    grad_ref, end_ref, arrived, leaving, send_sem, recv_sem, carry_ref=None, first=0, last=RING - 1, pace=1
):
    me, place, targets = ring_neighbours()
    rows, half = grad_ref.shape[0] // RING, grad_ref.shape[1] // 2
    piece_rows = rows // PIECES
    whole = last == RING - 1

    def grad_at(owner, piece, way):
        start = pl.multiple_of(owner * rows + piece * piece_rows, piece_rows)
        return grad_ref.at[pl.ds(start, piece_rows), pl.ds(way * half, half)]

    copies = {}
    for step in range(first, last):
        for piece in range(PIECES):
            for way in range(2):
                shift = RING - 1 - step if way == 0 else 1 + step
                source = grad_at(ring_device((place + shift) % RING), piece, way)
                if step:
                    if step > first:
                        copies[step - 1, piece, way].wait_recv()
                        come = arrived[step - 1, piece, way]
                    else:
                        come = carry_ref[piece, way]
                    running = come.astype(jnp.float32) + source[...].astype(jnp.float32)
                    leaving[step, piece, way] = running.astype(jnp.bfloat16)
                    source = leaving.at[step, piece, way]
                into = arrived.at[step, piece, way]
                if step == last - 1 and not whole:
                    into = end_ref.at[piece, way]
                copy = pltpu.make_async_remote_copy(
                    src_ref=source,
                    dst_ref=into,
                    send_sem=send_sem.at[step, piece, way],
                    recv_sem=recv_sem.at[step, piece, way],
                    device_id={"dp": targets[way]},
                    device_id_type=MESH,
                )
                copy.start()
                copies[step, piece, way] = copy
        for turn in range(pace):
            yield
    for piece in range(PIECES):
        for way in range(2):
            copies[last - 1, piece, way].wait_recv()
            if whole:
                total = arrived[last - 1, piece, way].astype(jnp.float32)
                total += grad_at(me, piece, way)[...].astype(jnp.float32)
                end_ref[pl.ds(piece * piece_rows, piece_rows), pl.ds(way * half, half)] = total
    for copy in copies.values():
        copy.wait_send()


def small_steps(small_ref, small_out_ref, small_slots, small_send, small_recv):
    me = lax.axis_index("dp")
    small_copies = []
    for shift in range(1, RING):
        copy = pltpu.make_async_remote_copy(
            src_ref=small_ref,
            dst_ref=small_slots.at[me],
            send_sem=small_send.at[shift - 1],
            recv_sem=small_recv.at[shift - 1],
            device_id={"dp": (me + shift) % RING},
            device_id_type=MESH,
        )
        copy.start()
        small_copies.append(copy)
    for turn in range(4):
        yield
    for copy in small_copies:
        copy.wait_recv()
    small_slots[me] = small_ref[...]
    small_total = small_slots[0]
    for index in range(1, RING):
        small_total += small_slots[index]
    small_out_ref[...] = small_total
    for copy in small_copies:
        copy.wait_send()


def tensor_partners():
    me = lax.axis_index("tensor")
    return me + 1 - 2 * (me % 2), (me + 2) % 4


def sum_steps(part_ref, sum_ref, near, chip_sum, far, total, send_sem, recv_sem):
    core = lax.axis_index("tensor") % 2
    partner, across = tensor_partners()
    half = part_ref.shape[0] // 2
    size = half // PARTS

    def rows_of(side, piece):
        return pl.ds(pl.multiple_of(side * half + piece * size, size), size)

    def send(source, target, stage, piece, device):
        copy = pltpu.make_async_remote_copy(
            src_ref=source,
            dst_ref=target,
            send_sem=send_sem.at[stage, piece],
            recv_sem=recv_sem.at[stage, piece],
            device_id={"tensor": device},
            device_id_type=MESH,
        )
        copy.start()
        return copy

    first = [
        send(part_ref.at[rows_of(1 - core, piece)], near.at[piece], 0, piece, partner)
        for piece in range(PARTS)
    ]
    second = []
    for piece in range(PARTS):
        first[piece].wait_recv()
        chip = near[piece].astype(jnp.float32) + part_ref[rows_of(core, piece)].astype(jnp.float32)
        chip_sum[piece] = chip.astype(jnp.bfloat16)
        second.append(send(chip_sum.at[piece], far.at[piece], 1, piece, across))
    yield
    third = []
    for piece in range(PARTS):
        second[piece].wait_recv()
        both = chip_sum[piece].astype(jnp.float32) + far[piece].astype(jnp.float32)
        total[piece] = both.astype(jnp.bfloat16)
        third.append(send(total.at[piece], sum_ref.at[rows_of(core, piece)], 2, piece, partner))
        if piece % 2:
            yield
    for piece in range(PARTS):
        third[piece].wait_recv()
        sum_ref[rows_of(core, piece)] = total[piece]
    for copy in first + second + third:
        copy.wait_send()


def take_turns(*plans):
    plans = list(plans)
    while plans:
        for plan in list(plans):
            if next(plan, "done") == "done":
                plans.remove(plan)


def greet_all(ring=(), tensor=()):
    barrier = pltpu.get_barrier_semaphore()
    for axis, devices in (("dp", ring), ("tensor", tensor)):
        for device in devices:
            pl.semaphore_signal(barrier, inc=1, device_id={axis: device}, device_id_type=MESH)
    pl.semaphore_wait(barrier, len(ring) + len(tensor))


def first_gather_kernel(in_ref, out_ref, full_ref, rest_ref, wide, share, rest, *sems):
    width = in_ref.shape[2]
    for index in range(12):
        if index == 3 or index >= 8:
            block = out_ref[0 if index == 3 else index - 7].T
        else:
            block = in_ref[index if index < 3 else index - 1]
        wide[:, index * width : (index + 1) * width] = block
    share[...] = wide[:, : 4 * width].astype(jnp.bfloat16)
    rest[...] = wide[:, 4 * width :].astype(jnp.bfloat16)
    greet_all(ring_neighbours()[2])
    take_turns(
        gather_steps(share, full_ref, *sems[:3]),
        gather_steps(rest, rest_ref, *sems[3:], last=GATHER_SPLIT, pace=2),
    )


def second_gather_kernel(share_ref, part_ref, full_ref, sum_ref, *scratch):
    greet_all(ring_neighbours()[2], tensor_partners())
    take_turns(
        gather_steps(share_ref, full_ref, *scratch[:3], first=GATHER_SPLIT),
        sum_steps(part_ref, sum_ref, *scratch[3:]),
    )


def sum_kernel(part_ref, sum_ref, *scratch):
    greet_all((), tensor_partners())
    take_turns(sum_steps(part_ref, sum_ref, *scratch))


def first_scatter_kernel(grad_ref, part_ref, carry_ref, sum_ref, *scratch):
    greet_all(ring_neighbours()[2], tensor_partners())
    take_turns(
        scatter_steps(grad_ref, carry_ref, *scratch[:4], last=SCATTER_SPLIT),
        sum_steps(part_ref, sum_ref, *scratch[4:]),
    )


def second_scatter_kernel(
    grad_ref,
    rest_ref,
    carry_ref,
    part_ref,
    small_ref,
    share_ref,
    rest_share_ref,
    sum_ref,
    small_out_ref,
    *scratch,
):
    me = lax.axis_index("dp")
    greet_all([(me + shift) % RING for shift in range(1, RING)], tensor_partners())
    take_turns(
        scatter_steps(grad_ref, share_ref, *scratch[:4]),
        sum_steps(part_ref, sum_ref, *scratch[4:10]),
        scatter_steps(
            rest_ref,
            rest_share_ref,
            *scratch[13:],
            carry_ref=carry_ref,
            first=SCATTER_SPLIT,
            pace=2,
        ),
        small_steps(small_ref, small_out_ref, *scratch[10:13]),
    )


def gather_scratch():
    shape = (RING - 1, PIECES, 2)
    sems = pltpu.SemaphoreType.DMA(shape)
    return [pltpu.SemaphoreType.DMA((2 * RING,)), sems, sems]


def scatter_scratch(rows, columns):
    shape = (RING - 1, PIECES, 2)
    slots = pltpu.VMEM(shape + (rows // PIECES, columns // 2), jnp.bfloat16)
    return [slots, slots, pltpu.SemaphoreType.DMA(shape), pltpu.SemaphoreType.DMA(shape)]


def small_scratch(small):
    sems = pltpu.SemaphoreType.DMA((RING - 1,))
    return [pltpu.VMEM((RING,) + small.shape, jnp.float32), sems, sems]


def sum_scratch(rows, columns):
    slots = pltpu.VMEM((PARTS, rows // (2 * PARTS), columns), jnp.bfloat16)
    sems = pltpu.SemaphoreType.DMA((3, PARTS))
    return [slots, slots, slots, slots, sems, sems]


def kernel_call(kernel, operands, results, scratch, collective_id):
    vmem = pl.BlockSpec(memory_space=pltpu.VMEM)
    extra = {} if collective_id is None else {"collective_id": collective_id, "has_side_effects": True}
    return pl.pallas_call(
        kernel,
        out_shape=tuple(jax.ShapeDtypeStruct(shape, dtype) for shape, dtype in results),
        in_specs=[vmem] * len(operands),
        out_specs=(vmem,) * len(results),
        scratch_shapes=scratch,
        compiler_params=pltpu.CompilerParams(**extra),
    )(*operands)


def ring_here(rows):
    return (
        lax.axis_size("dp") == RING
        and lax.axis_size("tensor") == 4
        and rows % 32 == 0
    )


def gather_first(in_weight, out_weight):
    rows, group_width = in_weight.shape[1:]
    if ring_here(rows):
        return kernel_call(
            first_gather_kernel,
            (in_weight, out_weight),
            [
                ((RING * rows, 4 * group_width), jnp.bfloat16),
                ((RING * rows, 8 * group_width), jnp.bfloat16),
            ],
            [
                pltpu.VMEM((rows, 12 * group_width), jnp.float32),
                pltpu.VMEM((rows, 4 * group_width), jnp.bfloat16),
                pltpu.VMEM((rows, 8 * group_width), jnp.bfloat16),
            ]
            + gather_scratch()
            + gather_scratch(),
            0,
        )
    in_low = in_weight.astype(jnp.bfloat16)
    out_low = out_weight.astype(jnp.bfloat16).swapaxes(1, 2)
    share = jnp.concatenate(list(in_low[:3]) + [out_low[0]], 1)
    rest = jnp.concatenate(list(in_low[3:]) + list(out_low[1:]), 1)
    return lax.all_gather(share, "dp", axis=0, tiled=True), rest


def plain_sum(part):
    if lax.axis_size("tensor") == 4 and part.shape[0] % 128 == 0:
        results = [(part.shape, jnp.bfloat16)]
        return kernel_call(sum_kernel, (part,), results, sum_scratch(*part.shape), 1)[0]
    return lax.psum(part, "tensor")


def gather_second(rows, rest, part):
    if ring_here(rows):
        return kernel_call(
            second_gather_kernel,
            (rest, part),
            [(rest.shape, jnp.bfloat16), (part.shape, jnp.bfloat16)],
            gather_scratch() + sum_scratch(*part.shape),
            2,
        )
    return lax.all_gather(rest, "dp", axis=0, tiled=True), lax.psum(part, "tensor")


def scatter_plain(grads):
    share = lax.psum_scatter(grads, "dp", scatter_dimension=0, tiled=True)
    return share.astype(jnp.float32)


def scatter_first(grads, part):
    rows, columns = grads.shape[0] // lax.axis_size("dp"), grads.shape[1]
    if ring_here(rows):
        return kernel_call(
            first_scatter_kernel,
            (grads, part),
            [
                ((PIECES, 2, rows // PIECES, columns // 2), jnp.bfloat16),
                (part.shape, jnp.bfloat16),
            ],
            scatter_scratch(rows, columns) + sum_scratch(*part.shape),
            3,
        )
    return scatter_plain(grads), lax.psum(part, "tensor")


def scatter_second(grads, rest, carry, part, small):
    rows, columns = grads.shape[0] // lax.axis_size("dp"), grads.shape[1]
    if ring_here(rows):
        return kernel_call(
            second_scatter_kernel,
            (grads, rest, carry, part, small),
            [
                ((rows, columns), jnp.float32),
                ((rows, rest.shape[1]), jnp.float32),
                (part.shape, jnp.bfloat16),
                (small.shape, jnp.float32),
            ],
            scatter_scratch(rows, columns)
            + sum_scratch(*part.shape)
            + small_scratch(small)
            + scatter_scratch(rows, rest.shape[1]),
            4,
        )
    return scatter_plain(grads), carry, lax.psum(part, "tensor"), lax.psum(small, "dp")


def matmul(left_op, right_op):
    return jnp.dot(left_op, right_op, preferred_element_type=jnp.float32)


def inner_rows(left_op, right_op):
    return lax.dot_general(
        left_op, right_op, (((0,), (0,)), ((), ())), preferred_element_type=jnp.float32
    )


def times_transposed(left_op, right_op):
    return lax.dot_general(
        left_op, right_op, (((1,), (1,)), ((), ())), preferred_element_type=jnp.float32
    )


def layer_norm(summed_rows, gain_vec, shift_vec):
    center = jnp.mean(summed_rows, -1, keepdims=True)
    offset = summed_rows - center
    inverse = lax.rsqrt(jnp.mean(offset * offset, -1, keepdims=True) + norm_eps)
    normed = offset * inverse
    return (normed * gain_vec + shift_vec, normed, inverse)


def norm_back(upstream, normed, inverse, gain_vec):
    scaled = upstream * gain_vec
    return inverse * (
        scaled
        - jnp.mean(scaled, -1, keepdims=True)
        - normed * jnp.mean(scaled * normed, -1, keepdims=True)
    )


def gelu_value(pre_act):
    return 0.5 * pre_act * (1.0 + jax.scipy.special.erf(pre_act * root_half))


def gelu_slope(pre_act):
    return (
        0.5 * (1.0 + jax.scipy.special.erf(pre_act * root_half))
        + pre_act * jnp.exp(-0.5 * pre_act * pre_act) * normal_peak
    )


def score_block(query_heads, key_heads, length):
    seq_len = query_heads.shape[0]
    scale_factor = query_heads.shape[-1] ** (-0.5)
    scores = (
        jnp.einsum("qhe,khe->hqk", query_heads, key_heads, preferred_element_type=jnp.float32)
        * scale_factor
    )
    usable = lax.broadcasted_iota(jnp.int32, (1, 1, seq_len), 2) < length
    return jnp.where(usable, scores, masked_score)


def attend_forward(operands):
    query_heads, key_heads, value_heads, length = operands
    scores = score_block(query_heads, key_heads, length)
    highest = jnp.max(scores, -1, keepdims=True)
    log_total = highest + jnp.log(jnp.sum(jnp.exp(scores - highest), -1, keepdims=True))
    probs_low = jnp.exp(scores - log_total).astype(jnp.bfloat16)
    mixed_heads = jnp.einsum(
        "hqk,khe->qhe", probs_low, value_heads, preferred_element_type=jnp.float32
    )
    return (mixed_heads.astype(jnp.bfloat16), log_total)


def attend_backward(operands):
    query_heads, key_heads, value_heads, grad_heads, log_total, length = operands
    scale_factor = query_heads.shape[-1] ** (-0.5)
    scores = score_block(query_heads, key_heads, length)
    probs = jnp.exp(scores - log_total)
    probs_low = probs.astype(jnp.bfloat16)
    grad_probs = jnp.einsum(
        "qhe,khe->hqk", grad_heads, value_heads, preferred_element_type=jnp.float32
    )
    row_dot = jnp.sum(probs * grad_probs, -1, keepdims=True)
    grad_scores = (probs * (grad_probs - row_dot) * scale_factor).astype(jnp.bfloat16)
    grad_query = jnp.einsum(
        "hqk,khe->qhe", grad_scores, key_heads, preferred_element_type=jnp.float32
    )
    grad_keys = jnp.einsum(
        "hqk,qhe->khe", grad_scores, query_heads, preferred_element_type=jnp.float32
    )
    grad_values = jnp.einsum(
        "hqk,qhe->khe", probs_low, grad_heads, preferred_element_type=jnp.float32
    )
    return (grad_query, grad_keys, grad_values)


def adam_update(param, grad, moments, decay):
    first = beta_first * moments[0] + (1.0 - beta_first) * grad
    second = beta_second * moments[1] + (1.0 - beta_second) * grad * grad
    first_hat = first / (1.0 - beta_first**step_count)
    second_hat = second / (1.0 - beta_second**step_count)
    new_param = param - learn_rate * (first_hat / (jnp.sqrt(second_hat) + adam_eps) + decay * param)
    return (new_param, jnp.stack([first, second]))


def adam_store(param, grad, moments, decay, new_param, new_moments):
    first = beta_first * moments[0] + (1.0 - beta_first) * grad
    second = beta_second * moments[1] + (1.0 - beta_second) * grad * grad
    first_hat = first / (1.0 - beta_first**step_count)
    second_hat = second / (1.0 - beta_second**step_count)
    step = first_hat / (jnp.sqrt(second_hat) + adam_eps) + decay * param
    new_param[...] = param - learn_rate * step
    new_moments[0] = first
    new_moments[1] = second


def adam_kernel(share_ref, rest_ref, small_ref, *refs):
    params, moments = refs[:4], refs[4:8]
    grads, new_params, new_moments = refs[8:12], refs[12:16], refs[16:20]
    matrix_in, matrix_out = params[0], params[1]
    width = matrix_in.shape[2]
    for index in range(12):
        source, place = (share_ref, index) if index < 4 else (rest_ref, index - 4)
        grad = source[:, place * width : (place + 1) * width]
        if index == 3 or index >= 8:
            group, spot, grad = 1, (0 if index == 3 else index - 7), grad.T
        else:
            group, spot = 0, (index if index < 3 else index - 1)
        grads[group][spot] = grad
        adam_store(
            params[group][spot],
            grad,
            (moments[group][0, spot], moments[group][1, spot]),
            weight_decay,
            new_params[group].at[spot],
            new_moments[group].at[:, spot],
        )
    model_width = params[3].shape[1]
    for group, start in ((2, model_width), (3, 0)):
        grad = small_ref[:6, start : start + params[group].shape[1]]
        grads[group][...] = grad
        adam_store(
            params[group][...], grad, moments[group], 0.0, new_params[group], new_moments[group]
        )


def update_all(share, rest, small, params, moments):
    group_width, width = params[0].shape[2], params[3].shape[1]
    if ring_here(params[0].shape[1]):
        shapes = [(a.shape, jnp.float32) for a in params + params + moments]
        return kernel_call(adam_kernel, (share, rest, small) + params + moments, shapes, [], None)
    total = jnp.concatenate([share, rest], 1)
    blocks = [total[:, k * group_width : (k + 1) * group_width] for k in range(12)]
    grads = (
        jnp.stack(blocks[:3] + blocks[4:8]),
        jnp.stack([blocks[3]] + blocks[8:]).swapaxes(1, 2),
        small[:6, width : width + group_width],
        small[:6, :width],
    )
    decays = (weight_decay, weight_decay, 0.0, 0.0)
    news = [adam_update(*group) for group in zip(params, grads, moments, decays)]
    return grads + tuple(n[0] for n in news) + tuple(n[1] for n in news)


def local(
    tokens,
    cotangent,
    lengths,
    in_weight,
    out_weight,
    in_bias,
    norm_vec,
    in_moments,
    out_moments,
    bias_moments,
    norm_moments,
):
    seq_count, seq_len, width = tokens.shape
    row_count = seq_count * seq_len
    first_full, rest = gather_first(in_weight, out_weight)
    group_width = in_weight.shape[2]
    heads_here = group_width // HDIM
    w_qkv = first_full[:, : 3 * group_width]
    w_proj = first_full[:, 3 * group_width :]
    bias_up = in_bias[2:6].reshape(1, 4 * group_width)

    def split_heads(flat_rows):
        return flat_rows.reshape(seq_count, seq_len, heads_here, HDIM)

    flat_tokens = tokens.reshape(row_count, width)
    qkv = matmul(flat_tokens, w_qkv)
    query = (qkv[:, :group_width] + in_bias[0]).astype(jnp.bfloat16)
    keys_low = qkv[:, group_width : 2 * group_width].astype(jnp.bfloat16)
    values_low = (qkv[:, 2 * group_width :] + in_bias[1]).astype(jnp.bfloat16)
    mixed_heads, log_total = lax.map(
        attend_forward,
        (split_heads(query), split_heads(keys_low), split_heads(values_low), lengths),
    )
    mixed_flat = mixed_heads.reshape(row_count, group_width)
    attn_part = times_transposed(mixed_flat, w_proj).astype(jnp.bfloat16)
    second_full, attn_out = gather_second(in_weight.shape[1], rest, attn_part)
    w_up = second_full[:, : 4 * group_width]
    w_down = second_full[:, 4 * group_width :]
    hidden, normed_one, inverse_one = layer_norm(
        flat_tokens.astype(jnp.float32) + attn_out.astype(jnp.float32) + norm_vec[0], norm_vec[1], norm_vec[2]
    )
    hidden_low = hidden.astype(jnp.bfloat16)
    pre_act = matmul(hidden_low, w_up) + bias_up
    act_low = gelu_value(pre_act).astype(jnp.bfloat16)
    ffn_part = times_transposed(act_low, w_down).astype(jnp.bfloat16)
    ffn_out = plain_sum(ffn_part).astype(jnp.float32)
    out_rows, normed_two, inverse_two = layer_norm(
        hidden + ffn_out + norm_vec[3], norm_vec[4], norm_vec[5]
    )
    positions = lax.broadcasted_iota(jnp.int32, (seq_count, seq_len), 1)
    live_rows = (positions < lengths[:, None]).astype(jnp.float32).reshape(row_count, 1)
    grad_out = cotangent.reshape(row_count, width).astype(jnp.float32) * live_rows
    grad_two = norm_back(grad_out, normed_two, inverse_two, norm_vec[4])
    grad_two_low = grad_two.astype(jnp.bfloat16)
    grad_down = inner_rows(grad_two_low, act_low).astype(jnp.bfloat16)
    grad_act = matmul(grad_two_low, w_down)
    grad_pre = grad_act * gelu_slope(pre_act)
    grad_pre_low = grad_pre.astype(jnp.bfloat16)
    grad_up = inner_rows(hidden_low, grad_pre_low).astype(jnp.bfloat16)
    rest_grads = jnp.concatenate([grad_up, grad_down], 1)
    back_part = times_transposed(grad_pre_low, w_up).astype(jnp.bfloat16)
    carry, back_sum = scatter_first(rest_grads, back_part)
    grad_hidden = grad_two + back_sum.astype(jnp.float32)
    grad_one = norm_back(grad_hidden, normed_one, inverse_one, norm_vec[1])
    grad_one_low = grad_one.astype(jnp.bfloat16)
    grad_proj = inner_rows(grad_one_low, mixed_flat).astype(jnp.bfloat16)
    grad_mixed = matmul(grad_one_low, w_proj).astype(jnp.bfloat16)
    grad_query, grad_keys, grad_values = lax.map(
        attend_backward,
        (
            split_heads(query),
            split_heads(keys_low),
            split_heads(values_low),
            split_heads(grad_mixed),
            log_total,
            lengths,
        ),
    )
    grad_query = grad_query.reshape(row_count, group_width)
    grad_keys = grad_keys.reshape(row_count, group_width)
    grad_values = grad_values.reshape(row_count, group_width)
    qkv_grad_low = jnp.concatenate([grad_query, grad_keys, grad_values], 1).astype(jnp.bfloat16)
    input_part = times_transposed(qkv_grad_low, w_qkv).astype(jnp.bfloat16)
    grad_qkv = inner_rows(flat_tokens, qkv_grad_low).astype(jnp.bfloat16)
    first_grads = jnp.concatenate([grad_qkv, grad_proj], 1)
    bias_rows = jnp.concatenate(
        [jnp.sum(grad_query, 0), jnp.sum(grad_values, 0), jnp.sum(grad_pre, 0)]
    ).reshape(6, group_width)
    norm_rows = jnp.stack(
        [
            jnp.sum(grad_one, 0),
            jnp.sum(grad_hidden * normed_one, 0),
            jnp.sum(grad_hidden, 0),
            jnp.sum(grad_two, 0),
            jnp.sum(grad_out * normed_two, 0),
            jnp.sum(grad_out, 0),
        ]
    )
    small = jnp.pad(jnp.concatenate([norm_rows, bias_rows], 1), ((0, 2), (0, 64)))
    share_total, rest_total, input_sum, small_total = scatter_second(
        first_grads, rest_grads, carry, input_part, small
    )
    grad_input = grad_one + input_sum.astype(jnp.float32)
    params = (in_weight, out_weight, in_bias, norm_vec)
    moments = (in_moments, out_moments, bias_moments, norm_moments)
    updates = update_all(share_total, rest_total, small_total, params, moments)
    output = out_rows.astype(jnp.bfloat16).reshape(seq_count, seq_len, width)
    grad_tokens = grad_input.astype(jnp.bfloat16).reshape(seq_count, seq_len, width)
    return (
        output,
        grad_tokens,
    ) + tuple(updates)


def solution(mesh):
    in_specs = (
        P("dp", None, None),
        P("dp", None, None),
        P("dp"),
        P(None, "dp", "tensor"),
        P(None, "tensor", "dp"),
        P(None, "tensor"),
        P(),
        P(None, None, "dp", "tensor"),
        P(None, None, "tensor", "dp"),
        P(None, None, "tensor"),
        P(),
    )
    out_specs = (
        P("dp", None, None),
        P("dp", None, None),
        P(None, "dp", "tensor"),
        P(None, "tensor", "dp"),
        P(None, "tensor"),
        P(),
        P(None, "dp", "tensor"),
        P(None, "tensor", "dp"),
        P(None, "tensor"),
        P(),
        P(None, None, "dp", "tensor"),
        P(None, None, "tensor", "dp"),
        P(None, None, "tensor"),
        P(),
    )
    return jax.shard_map(local, mesh=mesh, in_specs=in_specs, out_specs=out_specs, check_vma=False)
```
